32 devices in a mesh: layer: 8 (over y, x, core), dp: 4 (over z).
Axes of the slice: x: 2, y: 2, z: 4, core: 2. Of those that a mesh axis runs over, the one named last changes fastest.
Arguments:
- images: float32 [8, 16, 16, 128], P('dp'), may hold values from -6 to 6
- weights: bfloat16 [32, 3, 3, 128, 128], P('layer'), may hold values from -0.1875 to 0.1875
- biases: float32 [32, 128], P('layer'), may hold values from -3 to 3
- end_grad: float32 [8, 16, 16, 128], P('dp'), may hold values from -6 to 6
Outputs:
- interval_ends: float32 [8, 8, 16, 16, 128], P('layer', 'dp')
- start_adjoint: float32 [8, 8, 16, 16, 128], P('layer', 'dp')
- weight_grad: float32 [32, 3, 3, 128, 128], P('layer')
- bias_grad: float32 [32, 128], P('layer')
The draws below stay inside these ranges and needn't reach their ends.
All inputs are finite; a program needn't handle non-finite values.
Results may differ from the reference program's by a relative error of at most 0.012.
The reference program's roundings to bfloat16 on the way count: a program that leaves them out, or rounds other values in their place, can miss the bound.
Values sent between devices are 32-bit elements; how exact they have to be, the bound alone decides.
A program may use at most 128 MiB of HBM per device.

```python
import jax
import jax.numpy as jnp
from jax import lax

C = 128
H = 16
W = 16
BLK = 4
LAYERS = 32
IMAGES = 8
N_LAYER = 8


def steps_of(own_key, shape, split, least, high):
    loudness = 1.0
    for axis_at, blocks in split:
        draws = jax.random.uniform(jax.random.fold_in(jax.random.fold_in(own_key, 6), axis_at), (blocks,), jnp.float32, least / len(split), high / len(split))
        loudness = loudness * jnp.repeat(jnp.exp(draws), shape[axis_at] // blocks).reshape((-1,) + (1,) * (len(shape) - 1 - axis_at))
    return loudness


def noise(stream_key, shape, spread, limit, cuts=(), kind=jnp.bfloat16):
    loudness = steps_of(stream_key, shape, cuts, -0.22, 0.18) if cuts else 1.0
    drawn = jax.random.normal(stream_key, shape, jnp.float32) * spread * loudness
    return jnp.minimum(jnp.maximum(drawn, -limit), limit).astype(kind)


def setup_inputs(seed: int = 0) -> dict:
    arg_keys = jax.random.split(jax.random.key(seed), 5)
    return {
        "images": noise(arg_keys[0], (IMAGES, H, W, C), 1.0, 6.0, ((0, 4),), jnp.float32),
        "weights": noise(arg_keys[1], (LAYERS, 3, 3, C, C), (9 * C) ** -0.5, 0.1875, ((0, 8),)),
        "biases": noise(arg_keys[2], (LAYERS, C), 0.5, 3.0, ((0, 8),), jnp.float32),
        "end_grad": noise(arg_keys[3], (IMAGES, H, W, C), 1.0, 6.0, ((0, 4),), jnp.float32),
    }


step_size = 0.25
conv_layout = ('NHWC', 'HWIO', 'NHWC')

def convolve(states, kernel):
    return lax.conv_general_dilated(states.astype(jnp.bfloat16), kernel, (1, 1), 'SAME', dimension_numbers=conv_layout, preferred_element_type=jnp.float32)

def advance(states, weights, biases):
    inputs = []
    slopes = []
    for index in range(weights.shape[0]):
        preact = convolve(states, weights[index]) + biases[index]
        activation = jnp.tanh(preact)
        inputs.append(states.astype(jnp.bfloat16))
        slopes.append(activation)
        states = states + step_size * activation
    return (states, inputs, slopes)

def retreat(adjoint, transposed, slopes):
    for index in reversed(range(len(slopes))):
        change = step_size * (1.0 - slopes[index] * slopes[index]) * adjoint
        adjoint = adjoint + convolve(change, transposed[index])
    return adjoint

def kernel_grad(inputs_low, change_low):
    padded = jnp.pad(inputs_low, ((0, 0), (1, 1), (1, 1), (0, 0))).astype(jnp.float32)
    change_wide = change_low.astype(jnp.float32)
    height = change_low.shape[1]
    width = change_low.shape[2]
    taps = []
    for row_at in range(3):
        line = []
        for col_at in range(3):
            window = padded[:, row_at:row_at + height, col_at:col_at + width, :]
            line.append(jnp.einsum('bhwc,bhwd->cd', window, change_wide))
        taps.append(jnp.stack(line))
    return jnp.stack(taps)

def finish(adjoint, transposed, inputs, slopes):
    kernels = []
    offsets = []
    for index in reversed(range(len(slopes))):
        change = step_size * (1.0 - slopes[index] * slopes[index]) * adjoint
        change_low = change.astype(jnp.bfloat16)
        kernels.append(kernel_grad(inputs[index], change_low))
        offsets.append(lax.optimization_barrier(jnp.sum(change, axis=(0, 1, 2))))
        adjoint = adjoint + convolve(change_low, transposed[index])
    return (adjoint, jnp.stack(kernels[::-1]), jnp.stack(offsets[::-1]))

def coarse_chain(matrices, residues, backward):

    def advance_error(carried, pieces):
        matrix, residue = pieces
        return (jnp.einsum('bhwc,cd->bhwd', carried, matrix, precision=lax.Precision.HIGHEST) + residue, carried)
    _, result = lax.scan(advance_error, jnp.zeros_like(residues[0]), (matrices, residues), reverse=backward)
    return result

def apply_map(field, matrix):
    return jnp.einsum('bhwc,cd->bhwd', field, matrix, precision=lax.Precision.HIGHEST)

def reference(images, weights, biases, end_grad):
    kernels = weights.reshape(N_LAYER, BLK, 3, 3, C, C)
    offsets = biases.reshape(N_LAYER, BLK, C)
    transposed = jnp.swapaxes(jnp.flip(kernels, (2, 3)), 4, 5)
    matrices = jnp.eye(C, dtype=jnp.float32) + step_size * lax.optimization_barrier(jnp.sum(kernels[:, :, 1, 1].astype(jnp.float32), axis=1))
    guess = jax.vmap(apply_map, in_axes=(None, 0))(images, matrices)
    starts = jnp.concatenate([images[None], guess[:-1]], axis=0)
    relaxed, _, _ = jax.vmap(advance, in_axes=(0, 0, 0))(starts, kernels, offsets)
    error = coarse_chain(matrices, relaxed - guess, False)
    corrected = starts + error
    interval_ends, inputs, slopes = jax.vmap(advance, in_axes=(0, 0, 0))(corrected, kernels, offsets)
    back = jax.vmap(apply_map, in_axes=(None, 0))(end_grad, jnp.swapaxes(matrices, 1, 2))
    ends_adj = jnp.concatenate([back[1:], end_grad[None]], axis=0)
    again = jax.vmap(retreat, in_axes=(0, 0, 0))(ends_adj, transposed, slopes)
    adj_error = coarse_chain(jnp.swapaxes(matrices, 1, 2), again - back, True)
    start_adjoint, kernel_sums, offset_sums = jax.vmap(finish, in_axes=(0, 0, 0, 0))(ends_adj + adj_error, transposed, inputs, slopes)
    divisor = 1.0 / images.shape[0]
    weight_grad = kernel_sums.reshape(LAYERS, 3, 3, C, C) * divisor
    bias_grad = offset_sums.reshape(LAYERS, C) * divisor
    return (interval_ends, start_adjoint, weight_grad, bias_grad)
```

```python
import functools

import jax
import jax.numpy as jnp
from jax import lax
from jax.experimental import pallas as pl
from jax.experimental.pallas import tpu as pltpu
from jax.sharding import PartitionSpec as P

step_size = 0.25
MESH = pl.DeviceIdType.MESH
low = jnp.bfloat16


def dot(a, b, contract=((1,), (0,))):
    return lax.dot_general(a, b, (contract, ((), ())), preferred_element_type=jnp.float32)


NT = ((1,), (1,))
TN = ((0,), (0,))


def kernel(
    dims,
    images,
    weights,
    biases,
    end_grad,
    ends_out,
    start_out,
    wg_out,
    bg_out,
    flipped,
    window,
    maps,
    states_low,
    slopes,
    states_all,
    adj_all,
    residue,
    gathered,
    spread,
    error,
    map_send,
    map_recv,
    out_send,
    out_recv,
    back_send,
    back_recv,
    right_send,
    left_send,
    line_recv,
):
    groups, parts, count, height, width, images_all = dims
    rows, channels = images.shape
    blocks = weights.shape[0]
    share = rows // groups
    me = lax.axis_index("layer")
    z = lax.axis_index("dp")
    not_first = z > 0
    not_last = z < parts - 1

    def others(body):
        def step(ahead, _):
            body(ahead, lax.rem(me + ahead, groups))
            return 0

        lax.fori_loop(1, groups, step, 0)

    barrier = pltpu.get_barrier_semaphore()
    others(lambda ahead, to: pl.semaphore_signal(barrier, inc=1, device_id={"layer": to}, device_id_type=MESH))

    @pl.when(not_first)
    def _():
        pl.semaphore_signal(barrier, inc=1, device_id={"dp": z - 1}, device_id_type=MESH)

    @pl.when(not_last)
    def _():
        pl.semaphore_signal(barrier, inc=1, device_id={"dp": z + 1}, device_id_type=MESH)

    centre = slice(4 * channels, 5 * channels)
    total = weights[0, centre, :].astype(jnp.float32)
    for n in range(1, blocks):
        total = total + weights[n, centre, :].astype(jnp.float32)
    maps[me] = step_size * total

    neighbours = jnp.where(not_first, 1, 0) + jnp.where(not_last, 1, 0)
    pl.semaphore_wait(barrier, groups - 1 + neighbours)

    def map_copy(slot, to):
        return pltpu.make_async_remote_copy(
            src_ref=maps.at[slot],
            dst_ref=maps.at[slot],
            send_sem=map_send.at[to],
            recv_sem=map_recv.at[slot],
            device_id={"layer": to},
            device_id_type=MESH,
        )

    last = groups - 1
    after = lax.rem(me + 1, groups)
    before = lax.rem(me + last, groups)
    map_copy(me, after).start()

    def send_rest(ahead, _):
        map_copy(me, lax.rem(me + groups + 1 - ahead, groups)).start()
        return 0

    lax.fori_loop(2, groups, send_rest, 0)

    zero_row = jnp.zeros((count, 1, width, 3 * channels), low)
    window[:, 0:1] = zero_row
    window[:, height + 1 : height + 2] = zero_row

    def prepare(n, _):
        for tap in range(9):
            flipped[n, :, tap * channels : (tap + 1) * channels] = weights[
                n, (8 - tap) * channels : (9 - tap) * channels, :
            ]
        wg_out[n] = jnp.zeros(wg_out.shape[1:], jnp.float32)
        return 0

    lax.fori_loop(0, blocks, prepare, 0)
    bg_out[...] = jnp.zeros(bg_out.shape, jnp.float32)

    column = lax.rem(lax.broadcasted_iota(jnp.int32, (rows, channels), 0), width)

    def patches(field):
        left = jnp.where(column == 0, 0.0, pltpu.roll(field, 1, 0))
        right = jnp.where(column == width - 1, 0.0, pltpu.roll(field, rows - 1, 0))
        shape = (count, height, width, channels)
        window[:, 1 : height + 1, :, 0:channels] = left.astype(low).reshape(shape)
        window[:, 1 : height + 1, :, channels : 2 * channels] = field.astype(low).reshape(shape)
        window[:, 1 : height + 1, :, 2 * channels : 3 * channels] = right.astype(low).reshape(shape)
        return jnp.concatenate(
            [window[:, i : i + height].reshape(rows, 3 * channels) for i in range(3)], axis=1
        )

    def apply_map(field, slot):
        return field + dot(field.astype(low), maps[slot].astype(low))

    def apply_flipped(field, slot):
        return field + dot(field.astype(low), maps[slot].astype(low), NT)

    def advance(n, state):
        return state + step_size * jnp.tanh(dot(patches(state), weights[n]) + biases[pl.ds(n, 1), :])

    def trajectory(part, state):
        def step(n, state):
            states_low[n, part] = state.astype(low)
            activation = jnp.tanh(dot(patches(state), weights[n]) + biases[pl.ds(n, 1), :])
            slopes[n, part] = activation
            return state + step_size * activation

        return lax.fori_loop(0, blocks, step, state)

    def change_of(n, part, adjoint):
        slope = slopes[n, part]
        return step_size * (1.0 - slope * slope) * adjoint

    def retreat(part, adjoint):
        def step(i, adjoint):
            n = blocks - 1 - i
            return adjoint + dot(patches(change_of(n, part, adjoint)), flipped[n], NT)

        return lax.fori_loop(0, blocks, step, adjoint)

    divisor = 1.0 / images_all

    def sweep(part, adjoint):
        def step(i, adjoint):
            n = blocks - 1 - i
            change = change_of(n, part, adjoint)
            bg_out[pl.ds(n, 1), :] += jnp.sum(change, axis=0, keepdims=True) * divisor
            spots = patches(change)
            adjoint = adjoint + dot(spots, flipped[n], NT)
            grads = dot(states_low[n, part], spots, TN) * divisor
            for tap in range(9):
                wg_out[n, (8 - tap) * channels : (9 - tap) * channels, :] += grads[
                    :, tap * channels : (tap + 1) * channels
                ]
            return adjoint

        return lax.fori_loop(0, blocks, step, adjoint)

    def rows_of(slot):
        return pl.ds(pl.multiple_of(slot * share, share), share)

    def out_copy(phase, source, to):
        return pltpu.make_async_remote_copy(
            src_ref=residue.at[phase, rows_of(to)],
            dst_ref=gathered.at[phase, source],
            send_sem=out_send.at[phase, to],
            recv_sem=out_recv.at[phase, source],
            device_id={"layer": to},
            device_id_type=MESH,
        )

    def back_copy(phase, source, to):
        return pltpu.make_async_remote_copy(
            src_ref=spread.at[phase, to],
            dst_ref=error.at[phase, rows_of(source)],
            send_sem=back_send.at[phase, to],
            recv_sem=back_recv.at[phase, source],
            device_id={"layer": to},
            device_id_type=MESH,
        )

    def chain_start(phase, value):
        residue[phase] = value
        others(lambda ahead, to: out_copy(phase, me, to).start())
        gathered[phase, me] = residue[phase, rows_of(me)]

    def chain_scan(phase):
        def step(i, carried):
            k = i if phase == 0 else groups - 1 - i

            @pl.when(k != me)
            def _():
                spread[phase, k] = carried
                back_copy(phase, me, k).start()
                out_copy(phase, k, me).wait_recv()

            @pl.when(k == me)
            def _():
                error[phase, rows_of(me)] = carried

            mapped = apply_map(carried, k) if phase == 0 else apply_flipped(carried, k)
            return mapped + gathered[phase, k]

        lax.fori_loop(0, groups, step, jnp.zeros((share, channels), jnp.float32))

    def chain_finish(phase):
        others(lambda ahead, to: back_copy(phase, to, me).wait_recv())
        return error[phase]

    line = (states_all, adj_all)

    def line_copy(which, block, to, sends):
        return pltpu.make_async_remote_copy(
            src_ref=line[which].at[block],
            dst_ref=line[which].at[block],
            send_sem=sends.at[which, block],
            recv_sem=line_recv.at[which, block],
            device_id={"dp": to},
            device_id_type=MESH,
        )

    def go_right(which, block):
        @pl.when(not_last)
        def _():
            line_copy(which, block, z + 1, right_send).start()

    def go_left(which, block):
        @pl.when(not_first)
        def _():
            line_copy(which, block, z - 1, left_send).start()

    def line_start(which):
        go_right(which, z)
        go_left(which, z)

    def line_round(which, away):
        @pl.when(z - away >= 0)
        def _():
            line_copy(which, z - away, z, right_send).wait_recv()
            go_right(which, z - away)

        @pl.when(z + away < parts)
        def _():
            line_copy(which, z + away, z, left_send).wait_recv()
            go_left(which, z + away)

    def nth_other(i):
        back_side = parts - 1 - z
        paired = jnp.where(z < back_side, z, back_side)
        near = i // 2 + 1
        near_part = jnp.where(i % 2 == 0, z - near, z + near)
        far = i - paired + 1
        far_part = jnp.where(z > back_side, z - far, z + far)
        return jnp.where(i < 2 * paired, near_part, far_part)

    def other_trajectory(i):
        part = nth_other(i)
        trajectory(part, states_all[part])

    start_image = images[...]

    @pl.when(me != 0)
    def _():
        map_copy(before, me).wait_recv()

    starts = jnp.where(me == 0, start_image, apply_map(start_image, jnp.where(me == 0, me, before)))
    relaxed = lax.fori_loop(0, blocks, advance, starts)
    chain_start(0, relaxed - apply_map(start_image, me))

    def wait_map(ahead, source):
        @pl.when((source != before) | (me == 0))
        def _():
            map_copy(source, me).wait_recv()

    others(wait_map)
    end = end_grad[...]
    ends_adj = jnp.where(me == last, end, apply_flipped(end, after))
    back = apply_flipped(end, me)
    chain_scan(0)
    corrected = starts + chain_finish(0)
    states_all[z] = corrected
    line_start(0)
    ends_out[...] = trajectory(z, corrected)

    chain_start(1, retreat(z, ends_adj) - back)
    if parts > 1:
        line_round(0, 1)
        other_trajectory(0)
    chain_scan(1)
    if parts > 2:
        line_round(0, 2)
        other_trajectory(1)
    adjoint = ends_adj + chain_finish(1)
    adj_all[z] = adjoint
    line_start(1)
    start_out[...] = sweep(z, adjoint)
    for i in range(2, parts - 1):
        line_round(0, i + 1)
        other_trajectory(i)
    for i in range(parts - 1):
        line_round(1, i + 1)
        part = nth_other(i)
        sweep(part, adj_all[part])

    def sent(ahead, to):
        map_copy(me, to).wait_send()
        for phase in range(2):
            out_copy(phase, me, to).wait_send()
            back_copy(phase, me, to).wait_send()

    others(sent)
    for which in range(2):
        for away in range(parts):

            @pl.when((z - away >= 0) & not_last)
            def _():
                line_copy(which, z - away, z + 1, right_send).wait_send()

            @pl.when((z + away < parts) & not_first)
            def _():
                line_copy(which, z + away, z - 1, left_send).wait_send()


def shards(images, weights, biases, end_grad):
    groups = lax.axis_size("layer")
    parts = lax.axis_size("dp")
    count, height, width, channels = images.shape
    blocks = weights.shape[0]
    rows = count * height * width
    dims = (groups, parts, count, height, width, count * parts)
    f32 = jnp.float32
    field = jax.ShapeDtypeStruct((rows, channels), f32)
    share = rows // groups
    dma = pltpu.SemaphoreType.DMA
    vmem = pl.BlockSpec(memory_space=pltpu.VMEM)
    ends, start, wg, bg = pl.pallas_call(
        functools.partial(kernel, dims),
        out_shape=(
            field,
            field,
            jax.ShapeDtypeStruct((blocks, 9 * channels, channels), f32),
            jax.ShapeDtypeStruct((blocks, channels), f32),
        ),
        in_specs=[vmem] * 4,
        out_specs=(vmem,) * 4,
        scratch_shapes=[
            pltpu.VMEM((blocks, channels, 9 * channels), low),
            pltpu.VMEM((count, height + 2, width, 3 * channels), low),
            pltpu.VMEM((groups, channels, channels), f32),
            pltpu.VMEM((blocks, parts, rows, channels), low),
            pltpu.VMEM((blocks, parts, rows, channels), f32),
            pltpu.VMEM((parts, rows, channels), f32),
            pltpu.VMEM((parts, rows, channels), f32),
            pltpu.VMEM((2, rows, channels), f32),
            pltpu.VMEM((2, groups, share, channels), f32),
            pltpu.VMEM((2, groups, share, channels), f32),
            pltpu.VMEM((2, rows, channels), f32),
            dma((groups,)),
            dma((groups,)),
            dma((2, groups)),
            dma((2, groups)),
            dma((2, groups)),
            dma((2, groups)),
            dma((2, parts)),
            dma((2, parts)),
            dma((2, parts)),
        ],
        compiler_params=pltpu.CompilerParams(
            collective_id=0, has_side_effects=True, vmem_limit_bytes=60000 * 1024
        ),
    )(
        images.reshape(rows, channels),
        weights.reshape(blocks, 9 * channels, channels),
        biases,
        end_grad.reshape(rows, channels),
    )
    shape = (1,) + images.shape
    return (ends.reshape(shape), start.reshape(shape), wg.reshape(weights.shape), bg)


def solution(mesh):
    in_specs = (
        P("dp", None, None, None),
        P("layer", None, None, None, None),
        P("layer", None),
        P("dp", None, None, None),
    )
    out_specs = (
        P("layer", "dp", None, None, None),
        P("layer", "dp", None, None, None),
        P("layer", None, None, None, None),
        P("layer", None),
    )
    return jax.shard_map(shards, mesh=mesh, in_specs=in_specs, out_specs=out_specs, check_vma=False)
```

```python
import functools

import jax
import jax.numpy as jnp
from jax import lax
from jax.experimental import pallas as pl
from jax.experimental.pallas import tpu as pltpu
from jax.sharding import PartitionSpec as P

step_size = 0.25
MESH = pl.DeviceIdType.MESH
low = jnp.bfloat16


def dot(a, b, contract=((1,), (0,))):
    return lax.dot_general(a, b, (contract, ((), ())), preferred_element_type=jnp.float32)


NT = ((1,), (1,))
TN = ((0,), (0,))


def kernel(
    dims,
    images_in,
    weights_in,
    biases_in,
    end_grad_in,
    ends_out,
    start_out,
    wg_out,
    bg_out,
    images,
    weights,
    biases,
    end_grad,
    load_sems,
    flipped,
    window,
    maps,
    states_low,
    slopes,
    states_all,
    adj_all,
    residue,
    gathered,
    spread,
    error,
    map_send,
    map_recv,
    hand_send,
    out_send,
    out_recv,
    back_send,
    back_recv,
    right_send,
    left_send,
    line_recv,
):
    groups, parts, count, height, width, images_all = dims
    rows, channels = images_in.shape
    blocks = weights_in.shape[0]
    share = rows // groups
    me = lax.axis_index("layer")
    z = lax.axis_index("dp")
    not_first = z > 0
    not_last = z < parts - 1

    def others(body):
        def step(ahead, _):
            body(ahead, lax.rem(me + ahead, groups))
            return 0

        lax.fori_loop(1, groups, step, 0)

    loads = [
        pltpu.make_async_copy(source, target, load_sems.at[i])
        for i, (source, target) in enumerate(
            ((weights_in, weights), (images_in, images), (biases_in, biases), (end_grad_in, end_grad))
        )
    ]
    for load in loads:
        load.start()
    barrier = pltpu.get_barrier_semaphore()
    others(lambda ahead, to: pl.semaphore_signal(barrier, inc=1, device_id={"layer": to}, device_id_type=MESH))

    @pl.when(not_first)
    def _():
        pl.semaphore_signal(barrier, inc=1, device_id={"dp": z - 1}, device_id_type=MESH)

    @pl.when(not_last)
    def _():
        pl.semaphore_signal(barrier, inc=1, device_id={"dp": z + 1}, device_id_type=MESH)

    for load in loads:
        load.wait()
    centre = slice(4 * channels, 5 * channels)
    total = weights[0, centre, :].astype(jnp.float32)
    for n in range(1, blocks):
        total = total + weights[n, centre, :].astype(jnp.float32)
    maps[me] = step_size * total

    neighbours = jnp.where(not_first, 1, 0) + jnp.where(not_last, 1, 0)
    pl.semaphore_wait(barrier, groups - 1 + neighbours)

    def map_copy(slot, to):
        return pltpu.make_async_remote_copy(
            src_ref=maps.at[slot],
            dst_ref=maps.at[slot],
            send_sem=map_send.at[to],
            recv_sem=map_recv.at[slot],
            device_id={"layer": to},
            device_id_type=MESH,
        )

    last = groups - 1
    after = lax.rem(me + 1, groups)
    before = lax.rem(me + last, groups)
    pair = 2 if groups % 2 == 0 else 1
    partner = me + 1 - 2 * lax.rem(me, 2) if pair == 2 else me

    def same_side(body):
        def step(ahead, _):
            body(lax.rem(me + pair * ahead, groups))
            return 0

        lax.fori_loop(1, groups // pair, step, 0)

    map_copy(me, after).start()
    if pair == 2:

        @pl.when(partner != after)
        def _():
            map_copy(me, partner).start()

    def send_map(to):
        if pair == 1:

            @pl.when(to != after)
            def _():
                map_copy(me, to).start()

        else:
            map_copy(me, to).start()

    same_side(send_map)

    def hand_copy(slot):
        return pltpu.make_async_remote_copy(
            src_ref=maps.at[slot],
            dst_ref=maps.at[slot],
            send_sem=hand_send.at[slot],
            recv_sem=map_recv.at[slot],
            device_id={"layer": partner},
            device_id_type=MESH,
        )

    def is_handed(slot):
        return lax.rem(slot + 1, groups) != partner

    def hand_on(slot):
        @pl.when((slot != before) | (me == 0))
        def _():
            map_copy(slot, me).wait_recv()

        if pair == 2:

            @pl.when(is_handed(slot))
            def _():
                hand_copy(slot).start()

    zero_row = jnp.zeros((count, 1, width, 3 * channels), low)
    window[:, 0:1] = zero_row
    window[:, height + 1 : height + 2] = zero_row

    def prepare(n, _):
        for tap in range(9):
            flipped[n, :, tap * channels : (tap + 1) * channels] = weights[
                n, (8 - tap) * channels : (9 - tap) * channels, :
            ]
        wg_out[n] = jnp.zeros(wg_out.shape[1:], jnp.float32)
        return 0

    lax.fori_loop(0, blocks, prepare, 0)
    bg_out[...] = jnp.zeros(bg_out.shape, jnp.float32)

    column = lax.rem(lax.broadcasted_iota(jnp.int32, (rows, channels), 0), width)

    def patches(field):
        left = jnp.where(column == 0, 0.0, pltpu.roll(field, 1, 0))
        right = jnp.where(column == width - 1, 0.0, pltpu.roll(field, rows - 1, 0))
        shape = (count, height, width, channels)
        window[:, 1 : height + 1, :, 0:channels] = left.astype(low).reshape(shape)
        window[:, 1 : height + 1, :, channels : 2 * channels] = field.astype(low).reshape(shape)
        window[:, 1 : height + 1, :, 2 * channels : 3 * channels] = right.astype(low).reshape(shape)
        return jnp.concatenate(
            [window[:, i : i + height].reshape(rows, 3 * channels) for i in range(3)], axis=1
        )

    def apply_map(field, slot):
        return field + dot(field.astype(low), maps[slot].astype(low))

    def apply_flipped(field, slot):
        return field + dot(field.astype(low), maps[slot].astype(low), NT)

    def advance(n, state):
        return state + step_size * jnp.tanh(dot(patches(state), weights[n]) + biases[pl.ds(n, 1), :])

    def trajectory(part, state):
        def step(n, state):
            states_low[n, part] = state.astype(low)
            activation = jnp.tanh(dot(patches(state), weights[n]) + biases[pl.ds(n, 1), :])
            slopes[n, part] = activation
            return state + step_size * activation

        return lax.fori_loop(0, blocks, step, state)

    def change_of(n, part, adjoint):
        slope = slopes[n, part]
        return step_size * (1.0 - slope * slope) * adjoint

    def retreat(part, adjoint):
        def step(i, adjoint):
            n = blocks - 1 - i
            return adjoint + dot(patches(change_of(n, part, adjoint)), flipped[n], NT)

        return lax.fori_loop(0, blocks, step, adjoint)

    divisor = 1.0 / images_all

    def sweep(part, adjoint):
        def step(i, adjoint):
            n = blocks - 1 - i
            change = change_of(n, part, adjoint)
            bg_out[pl.ds(n, 1), :] += jnp.sum(change, axis=0, keepdims=True) * divisor
            spots = patches(change)
            adjoint = adjoint + dot(spots, flipped[n], NT)
            grads = dot(states_low[n, part], spots, TN) * divisor
            for tap in range(9):
                wg_out[n, (8 - tap) * channels : (9 - tap) * channels, :] += grads[
                    :, tap * channels : (tap + 1) * channels
                ]
            return adjoint

        return lax.fori_loop(0, blocks, step, adjoint)

    def rows_of(slot):
        return pl.ds(pl.multiple_of(slot * share, share), share)

    def out_copy(phase, source, to):
        return pltpu.make_async_remote_copy(
            src_ref=residue.at[phase, rows_of(to)],
            dst_ref=gathered.at[phase, source],
            send_sem=out_send.at[phase, to],
            recv_sem=out_recv.at[phase, source],
            device_id={"layer": to},
            device_id_type=MESH,
        )

    def back_copy(phase, source, to):
        return pltpu.make_async_remote_copy(
            src_ref=spread.at[phase, to],
            dst_ref=error.at[phase, rows_of(source)],
            send_sem=back_send.at[phase, to],
            recv_sem=back_recv.at[phase, source],
            device_id={"layer": to},
            device_id_type=MESH,
        )

    def chain_start(phase, value):
        residue[phase] = value
        others(lambda ahead, to: out_copy(phase, me, to).start())
        gathered[phase, me] = residue[phase, rows_of(me)]

    def chain_scan(phase):
        def step(i, carried):
            k = i if phase == 0 else groups - 1 - i

            @pl.when(k != me)
            def _():
                spread[phase, k] = carried
                back_copy(phase, me, k).start()
                out_copy(phase, k, me).wait_recv()

            @pl.when(k == me)
            def _():
                error[phase, rows_of(me)] = carried

            mapped = apply_map(carried, k) if phase == 0 else apply_flipped(carried, k)
            return mapped + gathered[phase, k]

        lax.fori_loop(0, groups, step, jnp.zeros((share, channels), jnp.float32))

    def chain_finish(phase):
        others(lambda ahead, to: back_copy(phase, to, me).wait_recv())
        return error[phase]

    line = (states_all, adj_all)

    piece = rows // count

    def line_copy(which, block, part, to, sends):
        where = line[which].at[block, part * piece : (part + 1) * piece]
        return pltpu.make_async_remote_copy(
            src_ref=where,
            dst_ref=where,
            send_sem=sends.at[which, block, part],
            recv_sem=line_recv.at[which, block, part],
            device_id={"dp": to},
            device_id_type=MESH,
        )

    def go_right(which, block, part):
        @pl.when(not_last)
        def _():
            line_copy(which, block, part, z + 1, right_send).start()

    def go_left(which, block, part):
        @pl.when(not_first)
        def _():
            line_copy(which, block, part, z - 1, left_send).start()

    def line_start(which):
        for part in range(count):
            go_right(which, z, part)
            go_left(which, z, part)

    def line_round(which, away):
        for part in range(count):

            @pl.when(z - away >= 0)
            def _():
                line_copy(which, z - away, part, z, right_send).wait_recv()
                go_right(which, z - away, part)

            @pl.when(z + away < parts)
            def _():
                line_copy(which, z + away, part, z, left_send).wait_recv()
                go_left(which, z + away, part)

    def nth_other(i):
        back_side = parts - 1 - z
        paired = jnp.where(z < back_side, z, back_side)
        near = i // 2 + 1
        near_part = jnp.where(i % 2 == 0, z - near, z + near)
        far = i - paired + 1
        far_part = jnp.where(z > back_side, z - far, z + far)
        return jnp.where(i < 2 * paired, near_part, far_part)

    def other_trajectory(i):
        part = nth_other(i)
        trajectory(part, states_all[part])

    start_image = images[...]

    @pl.when(me != 0)
    def _():
        map_copy(before, me).wait_recv()

    starts = jnp.where(me == 0, start_image, apply_map(start_image, jnp.where(me == 0, me, before)))
    relaxed = lax.fori_loop(0, blocks, advance, starts)
    chain_start(0, relaxed - apply_map(start_image, me))

    same_side(hand_on)

    def wait_map(ahead, source):
        @pl.when((lax.rem(source - me + groups, pair) != 0) & ((source != before) | (me == 0)))
        def _():
            map_copy(source, me).wait_recv()

    if pair == 2:
        others(wait_map)
    end = end_grad[...]
    ends_adj = jnp.where(me == last, end, apply_flipped(end, after))
    back = apply_flipped(end, me)
    chain_scan(0)
    corrected = starts + chain_finish(0)
    states_all[z] = corrected
    line_start(0)
    ends_out[...] = trajectory(z, corrected)

    chain_start(1, retreat(z, ends_adj) - back)
    if parts > 1:
        line_round(0, 1)
        other_trajectory(0)
    chain_scan(1)
    if parts > 2:
        line_round(0, 2)
        other_trajectory(1)
    adjoint = ends_adj + chain_finish(1)
    adj_all[z] = adjoint
    line_start(1)
    start_out[...] = sweep(z, adjoint)
    for i in range(2, parts - 1):
        line_round(0, i + 1)
        other_trajectory(i)
    for i in range(parts - 1):
        line_round(1, i + 1)
        part = nth_other(i)
        sweep(part, adj_all[part])

    def map_sent(to):
        if pair == 1:

            @pl.when(to != after)
            def _():
                map_copy(me, to).wait_send()

        else:
            map_copy(me, to).wait_send()

            @pl.when(is_handed(to))
            def _():
                hand_copy(to).wait_send()

    map_copy(me, after).wait_send()
    if pair == 2:

        @pl.when(partner != after)
        def _():
            map_copy(me, partner).wait_send()

    same_side(map_sent)

    def sent(ahead, to):
        for phase in range(2):
            out_copy(phase, me, to).wait_send()
            back_copy(phase, me, to).wait_send()

    others(sent)
    for which in range(2):
        for away in range(parts):

            @pl.when((z - away >= 0) & not_last)
            def _():
                for part in range(count):
                    line_copy(which, z - away, part, z + 1, right_send).wait_send()

            @pl.when((z + away < parts) & not_first)
            def _():
                for part in range(count):
                    line_copy(which, z + away, part, z - 1, left_send).wait_send()


def shards(images, weights, biases, end_grad):
    groups = lax.axis_size("layer")
    parts = lax.axis_size("dp")
    count, height, width, channels = images.shape
    blocks = weights.shape[0]
    rows = count * height * width
    dims = (groups, parts, count, height, width, count * parts)
    f32 = jnp.float32
    share = rows // groups
    dma = pltpu.SemaphoreType.DMA
    vmem = pl.BlockSpec(memory_space=pltpu.VMEM)
    ends, start, wg, bg = pl.pallas_call(
        functools.partial(kernel, dims),
        out_shape=(
            pltpu.VMEM((rows, channels), f32),
            pltpu.VMEM((rows, channels), f32),
            pltpu.VMEM((blocks, 9 * channels, channels), f32),
            pltpu.VMEM((blocks, channels), f32),
        ),
        in_specs=[pl.BlockSpec(memory_space=pltpu.HBM)] * 4,
        out_specs=(vmem,) * 4,
        scratch_shapes=[
            pltpu.VMEM((rows, channels), f32),
            pltpu.VMEM((blocks, 9 * channels, channels), low),
            pltpu.VMEM((blocks, channels), f32),
            pltpu.VMEM((rows, channels), f32),
            dma((4,)),
            pltpu.VMEM((blocks, channels, 9 * channels), low),
            pltpu.VMEM((count, height + 2, width, 3 * channels), low),
            pltpu.VMEM((groups, channels, channels), f32),
            pltpu.VMEM((blocks, parts, rows, channels), low),
            pltpu.VMEM((blocks, parts, rows, channels), f32),
            pltpu.VMEM((parts, rows, channels), f32),
            pltpu.VMEM((parts, rows, channels), f32),
            pltpu.VMEM((2, rows, channels), f32),
            pltpu.VMEM((2, groups, share, channels), f32),
            pltpu.VMEM((2, groups, share, channels), f32),
            pltpu.VMEM((2, rows, channels), f32),
            dma((groups,)),
            dma((groups,)),
            dma((groups,)),
            dma((2, groups)),
            dma((2, groups)),
            dma((2, groups)),
            dma((2, groups)),
            dma((2, parts, count)),
            dma((2, parts, count)),
            dma((2, parts, count)),
        ],
        compiler_params=pltpu.CompilerParams(
            collective_id=0, has_side_effects=True, vmem_limit_bytes=61 << 20
        ),
    )(
        images.reshape(rows, channels),
        weights.reshape(blocks, 9 * channels, channels),
        biases,
        end_grad.reshape(rows, channels),
    )
    shape = (1,) + images.shape
    return (ends.reshape(shape), start.reshape(shape), wg.reshape(weights.shape), bg)


def solution(mesh):
    in_specs = (
        P("dp", None, None, None),
        P("layer", None, None, None, None),
        P("layer", None),
        P("dp", None, None, None),
    )
    out_specs = (
        P("layer", "dp", None, None, None),
        P("layer", "dp", None, None, None),
        P("layer", None, None, None, None),
        P("layer", None),
    )
    return jax.shard_map(shards, mesh=mesh, in_specs=in_specs, out_specs=out_specs, check_vma=False)
```

```python
import functools

import jax
import jax.numpy as jnp
from jax import lax
from jax.experimental import pallas as pl
from jax.experimental.pallas import tpu as pltpu
from jax.sharding import PartitionSpec as P

step_size = 0.25
MESH = pl.DeviceIdType.MESH
low = jnp.bfloat16


def dot(a, b, contract=((1,), (0,))):
    return lax.dot_general(a, b, (contract, ((), ())), preferred_element_type=jnp.float32)


NT = ((1,), (1,))
TN = ((0,), (0,))


def kernel(
    dims,
    images_in,
    weights_in,
    biases_in,
    end_grad_in,
    ends_out,
    start_out,
    wg_out,
    bg_out,
    images,
    weights,
    biases,
    end_grad,
    load_sems,
    flipped,
    window,
    maps,
    states_low,
    slopes,
    states_all,
    adj_all,
    residue,
    gathered,
    spread,
    error,
    map_send,
    map_recv,
    hand_send,
    out_send,
    out_recv,
    back_send,
    back_recv,
    right_send,
    left_send,
    line_recv,
):
    groups, parts, count, height, width, images_all = dims
    rows, channels = images_in.shape
    blocks = weights_in.shape[0]
    share = rows // groups
    me = lax.axis_index("layer")
    z = lax.axis_index("dp")
    not_first = z > 0
    not_last = z < parts - 1

    def others(body):
        def step(ahead, _):
            body(ahead, lax.rem(me + ahead, groups))
            return 0

        lax.fori_loop(1, groups, step, 0)

    loads = [
        pltpu.make_async_copy(source, target, load_sems.at[i])
        for i, (source, target) in enumerate(
            ((weights_in, weights), (images_in, images), (biases_in, biases), (end_grad_in, end_grad))
        )
    ]
    for load in loads:
        load.start()
    barrier = pltpu.get_barrier_semaphore()
    others(lambda ahead, to: pl.semaphore_signal(barrier, inc=1, device_id={"layer": to}, device_id_type=MESH))

    @pl.when(not_first)
    def _():
        pl.semaphore_signal(barrier, inc=1, device_id={"dp": z - 1}, device_id_type=MESH)

    @pl.when(not_last)
    def _():
        pl.semaphore_signal(barrier, inc=1, device_id={"dp": z + 1}, device_id_type=MESH)

    for load in loads:
        load.wait()
    centre = slice(4 * channels, 5 * channels)
    total = weights[0, centre, :].astype(jnp.float32)
    for n in range(1, blocks):
        total = total + weights[n, centre, :].astype(jnp.float32)
    maps[me] = step_size * total

    neighbours = jnp.where(not_first, 1, 0) + jnp.where(not_last, 1, 0)
    pl.semaphore_wait(barrier, groups - 1 + neighbours)

    def map_copy(slot, to):
        return pltpu.make_async_remote_copy(
            src_ref=maps.at[slot],
            dst_ref=maps.at[slot],
            send_sem=map_send.at[to],
            recv_sem=map_recv.at[slot],
            device_id={"layer": to},
            device_id_type=MESH,
        )

    last = groups - 1
    after = lax.rem(me + 1, groups)
    before = lax.rem(me + last, groups)
    pair = 2 if groups % 2 == 0 else 1
    partner = me + 1 - 2 * lax.rem(me, 2) if pair == 2 else me

    def same_side(body):
        def step(ahead, _):
            body(lax.rem(me + pair * ahead, groups))
            return 0

        lax.fori_loop(1, groups // pair, step, 0)

    map_copy(me, after).start()
    if pair == 2:

        @pl.when(partner != after)
        def _():
            map_copy(me, partner).start()

    def send_map(to):
        if pair == 1:

            @pl.when(to != after)
            def _():
                map_copy(me, to).start()

        else:
            map_copy(me, to).start()

    same_side(send_map)

    def hand_copy(slot):
        return pltpu.make_async_remote_copy(
            src_ref=maps.at[slot],
            dst_ref=maps.at[slot],
            send_sem=hand_send.at[slot],
            recv_sem=map_recv.at[slot],
            device_id={"layer": partner},
            device_id_type=MESH,
        )

    def is_handed(slot):
        return lax.rem(slot + 1, groups) != partner

    def hand_on(slot):
        @pl.when((slot != before) | (me == 0))
        def _():
            map_copy(slot, me).wait_recv()

        if pair == 2:

            @pl.when(is_handed(slot))
            def _():
                hand_copy(slot).start()

    zero_row = jnp.zeros((count, 1, width, 3 * channels), low)
    window[:, 0:1] = zero_row
    window[:, height + 1 : height + 2] = zero_row

    def prepare(n, _):
        for tap in range(9):
            flipped[n, :, tap * channels : (tap + 1) * channels] = weights[
                n, (8 - tap) * channels : (9 - tap) * channels, :
            ]
        wg_out[n] = jnp.zeros(wg_out.shape[1:], jnp.float32)
        return 0

    lax.fori_loop(0, blocks, prepare, 0)
    bg_out[...] = jnp.zeros(bg_out.shape, jnp.float32)

    column = lax.rem(lax.broadcasted_iota(jnp.int32, (rows, channels), 0), width)

    def patches(field):
        size = field.shape[0]
        some = size // (height * width)
        place = column[:size]
        left = jnp.where(place == 0, 0.0, pltpu.roll(field, 1, 0))
        right = jnp.where(place == width - 1, 0.0, pltpu.roll(field, size - 1, 0))
        shape = (some, height, width, channels)
        window[:some, 1 : height + 1, :, 0:channels] = left.astype(low).reshape(shape)
        window[:some, 1 : height + 1, :, channels : 2 * channels] = field.astype(low).reshape(shape)
        window[:some, 1 : height + 1, :, 2 * channels : 3 * channels] = right.astype(low).reshape(shape)
        return jnp.concatenate(
            [window[:some, i : i + height].reshape(size, 3 * channels) for i in range(3)], axis=1
        )

    def apply_map(field, slot):
        return field + dot(field.astype(low), maps[slot].astype(low))

    def apply_flipped(field, slot):
        return field + dot(field.astype(low), maps[slot].astype(low), NT)

    def advance(n, state):
        return state + step_size * jnp.tanh(dot(patches(state), weights[n]) + biases[pl.ds(n, 1), :])

    def trajectory(part, state):
        def step(n, state):
            states_low[n, part] = state.astype(low)
            activation = jnp.tanh(dot(patches(state), weights[n]) + biases[pl.ds(n, 1), :])
            slopes[n, part] = activation
            return state + step_size * activation

        return lax.fori_loop(0, blocks, step, state)

    def change_of(n, part, adjoint, at=0):
        slope = slopes[n, part, at : at + adjoint.shape[0]]
        return step_size * (1.0 - slope * slope) * adjoint

    def retreat(part, adjoint):
        def step(i, adjoint):
            n = blocks - 1 - i
            return adjoint + dot(patches(change_of(n, part, adjoint)), flipped[n], NT)

        return lax.fori_loop(0, blocks, step, adjoint)

    divisor = 1.0 / images_all

    def sweep(part, adjoint, at=0):
        def step(i, adjoint):
            n = blocks - 1 - i
            change = change_of(n, part, adjoint, at)
            bg_out[pl.ds(n, 1), :] += jnp.sum(change, axis=0, keepdims=True) * divisor
            spots = patches(change)
            adjoint = adjoint + dot(spots, flipped[n], NT)
            grads = dot(states_low[n, part, at : at + adjoint.shape[0]], spots, TN) * divisor
            for tap in range(9):
                wg_out[n, (8 - tap) * channels : (9 - tap) * channels, :] += grads[
                    :, tap * channels : (tap + 1) * channels
                ]
            return adjoint

        return lax.fori_loop(0, blocks, step, adjoint)

    def rows_of(slot):
        return pl.ds(pl.multiple_of(slot * share, share), share)

    def out_copy(phase, source, to):
        return pltpu.make_async_remote_copy(
            src_ref=residue.at[phase, rows_of(to)],
            dst_ref=gathered.at[phase, source],
            send_sem=out_send.at[phase, to],
            recv_sem=out_recv.at[phase, source],
            device_id={"layer": to},
            device_id_type=MESH,
        )

    def back_copy(phase, source, to):
        return pltpu.make_async_remote_copy(
            src_ref=spread.at[phase, to],
            dst_ref=error.at[phase, rows_of(source)],
            send_sem=back_send.at[phase, to],
            recv_sem=back_recv.at[phase, source],
            device_id={"layer": to},
            device_id_type=MESH,
        )

    def chain_start(phase, value):
        residue[phase] = value
        others(lambda ahead, to: out_copy(phase, me, to).start())
        gathered[phase, me] = residue[phase, rows_of(me)]

    def chain_scan(phase):
        def step(i, carried):
            k = i if phase == 0 else groups - 1 - i

            @pl.when(k != me)
            def _():
                spread[phase, k] = carried
                back_copy(phase, me, k).start()
                out_copy(phase, k, me).wait_recv()

            @pl.when(k == me)
            def _():
                error[phase, rows_of(me)] = carried

            mapped = apply_map(carried, k) if phase == 0 else apply_flipped(carried, k)
            return mapped + gathered[phase, k]

        lax.fori_loop(0, groups, step, jnp.zeros((share, channels), jnp.float32))

    def chain_finish(phase):
        others(lambda ahead, to: back_copy(phase, to, me).wait_recv())
        return error[phase]

    line = (states_all, adj_all)

    piece = rows // count

    def line_copy(which, block, part, to, sends):
        where = line[which].at[block, part * piece : (part + 1) * piece]
        return pltpu.make_async_remote_copy(
            src_ref=where,
            dst_ref=where,
            send_sem=sends.at[which, block, part],
            recv_sem=line_recv.at[which, block, part],
            device_id={"dp": to},
            device_id_type=MESH,
        )

    def go_right(which, block, part):
        @pl.when(not_last)
        def _():
            line_copy(which, block, part, z + 1, right_send).start()

    def go_left(which, block, part):
        @pl.when(not_first)
        def _():
            line_copy(which, block, part, z - 1, left_send).start()

    def line_start(which):
        for part in range(count):
            go_right(which, z, part)
            go_left(which, z, part)

    def line_round(which, away, pieces=range(count)):
        for part in pieces:

            @pl.when(z - away >= 0)
            def _():
                line_copy(which, z - away, part, z, right_send).wait_recv()
                go_right(which, z - away, part)

            @pl.when(z + away < parts)
            def _():
                line_copy(which, z + away, part, z, left_send).wait_recv()
                go_left(which, z + away, part)

    def nth_other(i):
        back_side = parts - 1 - z
        paired = jnp.where(z < back_side, z, back_side)
        near = i // 2 + 1
        near_part = jnp.where(i % 2 == 0, z - near, z + near)
        far = i - paired + 1
        far_part = jnp.where(z > back_side, z - far, z + far)
        return jnp.where(i < 2 * paired, near_part, far_part)

    def other_trajectory(i):
        part = nth_other(i)
        trajectory(part, states_all[part])

    start_image = images[...]

    @pl.when(me != 0)
    def _():
        map_copy(before, me).wait_recv()

    starts = jnp.where(me == 0, start_image, apply_map(start_image, jnp.where(me == 0, me, before)))
    relaxed = lax.fori_loop(0, blocks, advance, starts)
    chain_start(0, relaxed - apply_map(start_image, me))

    same_side(hand_on)

    def wait_map(ahead, source):
        @pl.when((lax.rem(source - me + groups, pair) != 0) & ((source != before) | (me == 0)))
        def _():
            map_copy(source, me).wait_recv()

    if pair == 2:
        others(wait_map)
    end = end_grad[...]
    ends_adj = jnp.where(me == last, end, apply_flipped(end, after))
    back = apply_flipped(end, me)
    chain_scan(0)
    corrected = starts + chain_finish(0)
    states_all[z] = corrected
    line_start(0)
    ends_out[...] = trajectory(z, corrected)

    chain_start(1, retreat(z, ends_adj) - back)
    if parts > 1:
        line_round(0, 1)
        other_trajectory(0)
    chain_scan(1)
    if parts > 2:
        line_round(0, 2)
        other_trajectory(1)
    adjoint = ends_adj + chain_finish(1)
    adj_all[z] = adjoint
    line_start(1)
    start_out[...] = sweep(z, adjoint)
    for i in range(2, parts - 1):
        line_round(0, i + 1)
        other_trajectory(i)
    for i in range(parts - 2):
        line_round(1, i + 1)
        part = nth_other(i)
        sweep(part, adj_all[part])
    if parts > 1:
        part = nth_other(parts - 2)
        for i in range(count):
            line_round(1, parts - 1, (i,))
            sweep(part, adj_all[part, i * piece : (i + 1) * piece], i * piece)

    def map_sent(to):
        if pair == 1:

            @pl.when(to != after)
            def _():
                map_copy(me, to).wait_send()

        else:
            map_copy(me, to).wait_send()

            @pl.when(is_handed(to))
            def _():
                hand_copy(to).wait_send()

    map_copy(me, after).wait_send()
    if pair == 2:

        @pl.when(partner != after)
        def _():
            map_copy(me, partner).wait_send()

    same_side(map_sent)

    def sent(ahead, to):
        for phase in range(2):
            out_copy(phase, me, to).wait_send()
            back_copy(phase, me, to).wait_send()

    others(sent)
    for which in range(2):
        for away in range(parts):

            @pl.when((z - away >= 0) & not_last)
            def _():
                for part in range(count):
                    line_copy(which, z - away, part, z + 1, right_send).wait_send()

            @pl.when((z + away < parts) & not_first)
            def _():
                for part in range(count):
                    line_copy(which, z + away, part, z - 1, left_send).wait_send()


def shards(images, weights, biases, end_grad):
    groups = lax.axis_size("layer")
    parts = lax.axis_size("dp")
    count, height, width, channels = images.shape
    blocks = weights.shape[0]
    rows = count * height * width
    dims = (groups, parts, count, height, width, count * parts)
    f32 = jnp.float32
    share = rows // groups
    dma = pltpu.SemaphoreType.DMA
    vmem = pl.BlockSpec(memory_space=pltpu.VMEM)
    ends, start, wg, bg = pl.pallas_call(
        functools.partial(kernel, dims),
        out_shape=(
            pltpu.VMEM((rows, channels), f32),
            pltpu.VMEM((rows, channels), f32),
            pltpu.VMEM((blocks, 9 * channels, channels), f32),
            pltpu.VMEM((blocks, channels), f32),
        ),
        in_specs=[pl.BlockSpec(memory_space=pltpu.HBM)] * 4,
        out_specs=(vmem,) * 4,
        scratch_shapes=[
            pltpu.VMEM((rows, channels), f32),
            pltpu.VMEM((blocks, 9 * channels, channels), low),
            pltpu.VMEM((blocks, channels), f32),
            pltpu.VMEM((rows, channels), f32),
            dma((4,)),
            pltpu.VMEM((blocks, channels, 9 * channels), low),
            pltpu.VMEM((count, height + 2, width, 3 * channels), low),
            pltpu.VMEM((groups, channels, channels), f32),
            pltpu.VMEM((blocks, parts, rows, channels), low),
            pltpu.VMEM((blocks, parts, rows, channels), f32),
            pltpu.VMEM((parts, rows, channels), f32),
            pltpu.VMEM((parts, rows, channels), f32),
            pltpu.VMEM((2, rows, channels), f32),
            pltpu.VMEM((2, groups, share, channels), f32),
            pltpu.VMEM((2, groups, share, channels), f32),
            pltpu.VMEM((2, rows, channels), f32),
            dma((groups,)),
            dma((groups,)),
            dma((groups,)),
            dma((2, groups)),
            dma((2, groups)),
            dma((2, groups)),
            dma((2, groups)),
            dma((2, parts, count)),
            dma((2, parts, count)),
            dma((2, parts, count)),
        ],
        compiler_params=pltpu.CompilerParams(
            collective_id=0, has_side_effects=True, vmem_limit_bytes=61 << 20
        ),
    )(
        images.reshape(rows, channels),
        weights.reshape(blocks, 9 * channels, channels),
        biases,
        end_grad.reshape(rows, channels),
    )
    shape = (1,) + images.shape
    return (ends.reshape(shape), start.reshape(shape), wg.reshape(weights.shape), bg)


def solution(mesh):
    in_specs = (
        P("dp", None, None, None),
        P("layer", None, None, None, None),
        P("layer", None),
        P("dp", None, None, None),
    )
    out_specs = (
        P("layer", "dp", None, None, None),
        P("layer", "dp", None, None, None),
        P("layer", None, None, None, None),
        P("layer", None),
    )
    return jax.shard_map(shards, mesh=mesh, in_specs=in_specs, out_specs=out_specs, check_vma=False)
```

```python
import functools

import jax
import jax.numpy as jnp
from jax import lax
from jax.experimental import pallas as pl
from jax.experimental.pallas import tpu as pltpu
from jax.sharding import PartitionSpec as P

step_size = 0.25
MESH = pl.DeviceIdType.MESH
low = jnp.bfloat16


def dot(a, b, contract=((1,), (0,))):
    return lax.dot_general(a, b, (contract, ((), ())), preferred_element_type=jnp.float32)


NT = ((1,), (1,))
TN = ((0,), (0,))


def kernel(
    dims,
    images_in,
    weights_in,
    biases_in,
    end_grad_in,
    both_out,
    wg_out,
    bg_out,
    images,
    weights,
    biases,
    end_grad,
    load_sems,
    flipped,
    window,
    maps,
    states_low,
    slopes,
    states_all,
    adj_all,
    residue,
    gathered,
    spread,
    error,
    map_send,
    map_recv,
    hand_send,
    out_send,
    out_recv,
    back_send,
    back_recv,
    right_send,
    left_send,
    line_recv,
):
    groups, parts, count, height, width, images_all = dims
    rows, channels = images_in.shape
    blocks = weights_in.shape[0]
    share = rows // groups
    me = lax.axis_index("layer")
    z = lax.axis_index("dp")
    not_first = z > 0
    not_last = z < parts - 1

    def others(body):
        def step(ahead, _):
            body(ahead, lax.rem(me + ahead, groups))
            return 0

        lax.fori_loop(1, groups, step, 0)

    loads = [
        pltpu.make_async_copy(source, target, load_sems.at[i])
        for i, (source, target) in enumerate(
            ((weights_in, weights), (images_in, images), (biases_in, biases), (end_grad_in, end_grad))
        )
    ]
    for load in loads:
        load.start()
    barrier = pltpu.get_barrier_semaphore()
    others(lambda ahead, to: pl.semaphore_signal(barrier, inc=1, device_id={"layer": to}, device_id_type=MESH))

    @pl.when(not_first)
    def _():
        pl.semaphore_signal(barrier, inc=1, device_id={"dp": z - 1}, device_id_type=MESH)

    @pl.when(not_last)
    def _():
        pl.semaphore_signal(barrier, inc=1, device_id={"dp": z + 1}, device_id_type=MESH)

    loads[0].wait()
    centre = slice(4 * channels, 5 * channels)
    total = weights[0, centre, :].astype(jnp.float32)
    for n in range(1, blocks):
        total = total + weights[n, centre, :].astype(jnp.float32)
    maps[me] = step_size * total

    neighbours = jnp.where(not_first, 1, 0) + jnp.where(not_last, 1, 0)
    pl.semaphore_wait(barrier, groups - 1 + neighbours)

    def map_copy(slot, to):
        return pltpu.make_async_remote_copy(
            src_ref=maps.at[slot],
            dst_ref=maps.at[slot],
            send_sem=map_send.at[to],
            recv_sem=map_recv.at[slot],
            device_id={"layer": to},
            device_id_type=MESH,
        )

    last = groups - 1
    after = lax.rem(me + 1, groups)
    before = lax.rem(me + last, groups)
    pair = 2 if groups % 2 == 0 else 1
    partner = me + 1 - 2 * lax.rem(me, 2) if pair == 2 else me

    def same_side(body):
        def step(ahead, _):
            body(lax.rem(me + pair * ahead, groups))
            return 0

        lax.fori_loop(1, groups // pair, step, 0)

    map_copy(me, after).start()
    if pair == 2:

        @pl.when(partner != after)
        def _():
            map_copy(me, partner).start()

    def send_map(to):
        if pair == 1:

            @pl.when(to != after)
            def _():
                map_copy(me, to).start()

        else:
            map_copy(me, to).start()

    same_side(send_map)

    def hand_copy(slot):
        return pltpu.make_async_remote_copy(
            src_ref=maps.at[slot],
            dst_ref=maps.at[slot],
            send_sem=hand_send.at[slot],
            recv_sem=map_recv.at[slot],
            device_id={"layer": partner},
            device_id_type=MESH,
        )

    def is_handed(slot):
        return lax.rem(slot + 1, groups) != partner

    def hand_on(slot):
        @pl.when((slot != before) | (me == 0))
        def _():
            map_copy(slot, me).wait_recv()

        if pair == 2:

            @pl.when(is_handed(slot))
            def _():
                hand_copy(slot).start()

    for load in loads[1:]:
        load.wait()

    zero_row = jnp.zeros((count, 1, width, 3 * channels), low)
    window[:, 0:1] = zero_row
    window[:, height + 1 : height + 2] = zero_row

    def prepare(n, _):
        for tap in range(9):
            flipped[n, :, tap * channels : (tap + 1) * channels] = weights[
                n, (8 - tap) * channels : (9 - tap) * channels, :
            ]
        wg_out[n] = jnp.zeros(wg_out.shape[1:], jnp.float32)
        return 0

    lax.fori_loop(0, blocks, prepare, 0)
    bg_out[...] = jnp.zeros(bg_out.shape, jnp.float32)

    column = lax.rem(lax.broadcasted_iota(jnp.int32, (rows, channels), 0), width)

    def patches(field):
        size = field.shape[0]
        some = size // (height * width)
        place = column[:size]
        left = jnp.where(place == 0, 0.0, pltpu.roll(field, 1, 0))
        right = jnp.where(place == width - 1, 0.0, pltpu.roll(field, size - 1, 0))
        shape = (some, height, width, channels)
        window[:some, 1 : height + 1, :, 0:channels] = left.astype(low).reshape(shape)
        window[:some, 1 : height + 1, :, channels : 2 * channels] = field.astype(low).reshape(shape)
        window[:some, 1 : height + 1, :, 2 * channels : 3 * channels] = right.astype(low).reshape(shape)
        return jnp.concatenate(
            [window[:some, i : i + height].reshape(size, 3 * channels) for i in range(3)], axis=1
        )

    def apply_map(field, slot):
        return field + dot(field.astype(low), maps[slot].astype(low))

    def apply_flipped(field, slot):
        return field + dot(field.astype(low), maps[slot].astype(low), NT)

    def advance(n, state):
        return state + step_size * jnp.tanh(dot(patches(state), weights[n]) + biases[pl.ds(n, 1), :])

    def trajectory(part, state):
        def step(n, state):
            states_low[n, part] = state.astype(low)
            activation = jnp.tanh(dot(patches(state), weights[n]) + biases[pl.ds(n, 1), :])
            slopes[n, part] = activation
            return state + step_size * activation

        return lax.fori_loop(0, blocks, step, state)

    def change_of(n, part, adjoint, at=0):
        slope = slopes[n, part, at : at + adjoint.shape[0]]
        return step_size * (1.0 - slope * slope) * adjoint

    def retreat(part, adjoint):
        def step(i, adjoint):
            n = blocks - 1 - i
            return adjoint + dot(patches(change_of(n, part, adjoint)), flipped[n], NT)

        return lax.fori_loop(0, blocks, step, adjoint)

    divisor = 1.0 / images_all

    def sweep(part, adjoint, at=0):
        def step(i, adjoint):
            n = blocks - 1 - i
            change = change_of(n, part, adjoint, at)
            bg_out[pl.ds(n, 1), :] += jnp.sum(change, axis=0, keepdims=True) * divisor
            spots = patches(change)
            adjoint = adjoint + dot(spots, flipped[n], NT)
            grads = dot(states_low[n, part, at : at + adjoint.shape[0]], spots, TN) * divisor
            for tap in range(9):
                wg_out[n, (8 - tap) * channels : (9 - tap) * channels, :] += grads[
                    :, tap * channels : (tap + 1) * channels
                ]
            return adjoint

        return lax.fori_loop(0, blocks, step, adjoint)

    def rows_of(slot):
        return pl.ds(pl.multiple_of(slot * share, share), share)

    def out_copy(phase, source, to):
        return pltpu.make_async_remote_copy(
            src_ref=residue.at[phase, rows_of(to)],
            dst_ref=gathered.at[phase, source],
            send_sem=out_send.at[phase, to],
            recv_sem=out_recv.at[phase, source],
            device_id={"layer": to},
            device_id_type=MESH,
        )

    def back_copy(phase, source, to):
        return pltpu.make_async_remote_copy(
            src_ref=spread.at[phase, to],
            dst_ref=error.at[phase, rows_of(source)],
            send_sem=back_send.at[phase, to],
            recv_sem=back_recv.at[phase, source],
            device_id={"layer": to},
            device_id_type=MESH,
        )

    def chain_start(phase, value):
        residue[phase] = value
        others(lambda ahead, to: out_copy(phase, me, to).start())
        gathered[phase, me] = residue[phase, rows_of(me)]

    def chain_scan(phase):
        def step(i, carried):
            k = i if phase == 0 else groups - 1 - i

            @pl.when(k != me)
            def _():
                spread[phase, k] = carried
                back_copy(phase, me, k).start()
                out_copy(phase, k, me).wait_recv()

            @pl.when(k == me)
            def _():
                error[phase, rows_of(me)] = carried

            mapped = apply_map(carried, k) if phase == 0 else apply_flipped(carried, k)
            return mapped + gathered[phase, k]

        lax.fori_loop(0, groups, step, jnp.zeros((share, channels), jnp.float32))

    def chain_finish(phase):
        others(lambda ahead, to: back_copy(phase, to, me).wait_recv())
        return error[phase]

    line = (states_all, adj_all)

    piece = rows // count

    def line_copy(which, block, part, to, sends):
        where = line[which].at[block, part * piece : (part + 1) * piece]
        return pltpu.make_async_remote_copy(
            src_ref=where,
            dst_ref=where,
            send_sem=sends.at[which, block, part],
            recv_sem=line_recv.at[which, block, part],
            device_id={"dp": to},
            device_id_type=MESH,
        )

    def go_right(which, block, part):
        @pl.when(not_last)
        def _():
            line_copy(which, block, part, z + 1, right_send).start()

    def go_left(which, block, part):
        @pl.when(not_first)
        def _():
            line_copy(which, block, part, z - 1, left_send).start()

    def line_start(which):
        for part in range(count):
            go_right(which, z, part)
            go_left(which, z, part)

    def line_round(which, away, pieces=range(count)):
        for part in pieces:

            @pl.when(z - away >= 0)
            def _():
                line_copy(which, z - away, part, z, right_send).wait_recv()
                go_right(which, z - away, part)

            @pl.when(z + away < parts)
            def _():
                line_copy(which, z + away, part, z, left_send).wait_recv()
                go_left(which, z + away, part)

    def nth_other(i):
        back_side = parts - 1 - z
        paired = jnp.where(z < back_side, z, back_side)
        near = i // 2 + 1
        near_part = jnp.where(i % 2 == 0, z - near, z + near)
        far = i - paired + 1
        far_part = jnp.where(z > back_side, z - far, z + far)
        return jnp.where(i < 2 * paired, near_part, far_part)

    def other_trajectory(i):
        part = nth_other(i)
        trajectory(part, states_all[part])

    start_image = images[...]

    @pl.when(me != 0)
    def _():
        map_copy(before, me).wait_recv()

    starts = jnp.where(me == 0, start_image, apply_map(start_image, jnp.where(me == 0, me, before)))
    relaxed = lax.fori_loop(0, blocks, advance, starts)
    chain_start(0, relaxed - apply_map(start_image, me))

    same_side(hand_on)

    def wait_map(ahead, source):
        @pl.when((lax.rem(source - me + groups, pair) != 0) & ((source != before) | (me == 0)))
        def _():
            map_copy(source, me).wait_recv()

    if pair == 2:
        others(wait_map)
    end = end_grad[...]
    ends_adj = jnp.where(me == last, end, apply_flipped(end, after))
    back = apply_flipped(end, me)
    chain_scan(0)
    corrected = starts + chain_finish(0)
    states_all[z] = corrected
    line_start(0)
    both_out[0] = trajectory(z, corrected)

    chain_start(1, retreat(z, ends_adj) - back)
    if parts > 1:
        line_round(0, 1)
        other_trajectory(0)
    chain_scan(1)
    if parts > 2:
        line_round(0, 2)
        other_trajectory(1)
    adjoint = ends_adj + chain_finish(1)
    adj_all[z] = adjoint
    line_start(1)
    both_out[1] = sweep(z, adjoint)
    for i in range(2, parts - 1):
        line_round(0, i + 1)
        other_trajectory(i)
    for i in range(parts - 2):
        line_round(1, i + 1)
        part = nth_other(i)
        sweep(part, adj_all[part])
    if parts > 1:
        part = nth_other(parts - 2)
        for i in range(count):
            line_round(1, parts - 1, (i,))
            sweep(part, adj_all[part, i * piece : (i + 1) * piece], i * piece)

    def map_sent(to):
        if pair == 1:

            @pl.when(to != after)
            def _():
                map_copy(me, to).wait_send()

        else:
            map_copy(me, to).wait_send()

            @pl.when(is_handed(to))
            def _():
                hand_copy(to).wait_send()

    map_copy(me, after).wait_send()
    if pair == 2:

        @pl.when(partner != after)
        def _():
            map_copy(me, partner).wait_send()

    same_side(map_sent)

    def sent(ahead, to):
        for phase in range(2):
            out_copy(phase, me, to).wait_send()
            back_copy(phase, me, to).wait_send()

    others(sent)
    for which in range(2):
        for away in range(parts):

            @pl.when((z - away >= 0) & not_last)
            def _():
                for part in range(count):
                    line_copy(which, z - away, part, z + 1, right_send).wait_send()

            @pl.when((z + away < parts) & not_first)
            def _():
                for part in range(count):
                    line_copy(which, z + away, part, z - 1, left_send).wait_send()


def shards(images, weights, biases, end_grad):
    groups = lax.axis_size("layer")
    parts = lax.axis_size("dp")
    count, height, width, channels = images.shape
    blocks = weights.shape[0]
    rows = count * height * width
    dims = (groups, parts, count, height, width, count * parts)
    f32 = jnp.float32
    share = rows // groups
    dma = pltpu.SemaphoreType.DMA
    vmem = pl.BlockSpec(memory_space=pltpu.VMEM)
    both, wg, bg = pl.pallas_call(
        functools.partial(kernel, dims),
        out_shape=(
            pltpu.VMEM((2, rows, channels), f32),
            pltpu.VMEM((blocks, 9 * channels, channels), f32),
            pltpu.VMEM((blocks, channels), f32),
        ),
        in_specs=[pl.BlockSpec(memory_space=pltpu.HBM)] * 4,
        out_specs=(vmem,) * 3,
        scratch_shapes=[
            pltpu.VMEM((rows, channels), f32),
            pltpu.VMEM((blocks, 9 * channels, channels), low),
            pltpu.VMEM((blocks, channels), f32),
            pltpu.VMEM((rows, channels), f32),
            dma((4,)),
            pltpu.VMEM((blocks, channels, 9 * channels), low),
            pltpu.VMEM((count, height + 2, width, 3 * channels), low),
            pltpu.VMEM((groups, channels, channels), f32),
            pltpu.VMEM((blocks, parts, rows, channels), low),
            pltpu.VMEM((blocks, parts, rows, channels), f32),
            pltpu.VMEM((parts, rows, channels), f32),
            pltpu.VMEM((parts, rows, channels), f32),
            pltpu.VMEM((2, rows, channels), f32),
            pltpu.VMEM((2, groups, share, channels), f32),
            pltpu.VMEM((2, groups, share, channels), f32),
            pltpu.VMEM((2, rows, channels), f32),
            dma((groups,)),
            dma((groups,)),
            dma((groups,)),
            dma((2, groups)),
            dma((2, groups)),
            dma((2, groups)),
            dma((2, groups)),
            dma((2, parts, count)),
            dma((2, parts, count)),
            dma((2, parts, count)),
        ],
        compiler_params=pltpu.CompilerParams(
            collective_id=0, has_side_effects=True, vmem_limit_bytes=61 << 20
        ),
    )(
        images.reshape(rows, channels),
        weights.reshape(blocks, 9 * channels, channels),
        biases,
        end_grad.reshape(rows, channels),
    )
    shape = (1,) + images.shape
    return (both[0].reshape(shape), both[1].reshape(shape), wg.reshape(weights.shape), bg)


def solution(mesh):
    in_specs = (
        P("dp", None, None, None),
        P("layer", None, None, None, None),
        P("layer", None),
        P("dp", None, None, None),
    )
    out_specs = (
        P("layer", "dp", None, None, None),
        P("layer", "dp", None, None, None),
        P("layer", None, None, None, None),
        P("layer", None),
    )
    return jax.shard_map(shards, mesh=mesh, in_specs=in_specs, out_specs=out_specs, check_vma=False)
```
